128 devices in a mesh: grp: 4 (over z_hi, core), dev: 32 (over y, x, z_lo).
Axes of the slice: x: 4, y: 4, z: 4 (z_hi: 2, z_lo: 2; z = z_hi * 2 + z_lo), core: 2. Of those that a mesh axis runs over, the one named last changes fastest.
Arguments:
- layer_input: bfloat16 [262144, 1024], P(('grp', 'dev')), may hold values from -24 to 24
- hidden_pre: bfloat16 [262144, 1024], P(('grp', 'dev')), may hold values from -24 to 24
- out_grad: bfloat16 [262144, 512], P(('grp', 'dev')), may hold values from -6 to 6
- second_weight: bfloat16 [1024, 512], replicated, may hold values from -0.25 to 0.25
- row_grads: bfloat16 [262144, 128], P(('grp', 'dev')), may hold values from -6 to 6
- row_ids: int32 [262144], P(('grp', 'dev')), may hold values from 0 to 2047
- block_counts: int32 [4096], P(('grp', 'dev')), may hold values from 1 to 64, as said below
- emb_table: float32 [65536, 128], P('dev'), may hold values from -4 to 4
- adagrad_state: float32 [65536, 128], P('dev'), may hold values from 0.01 to 1
Outputs:
- grad_first: float32 [1024, 1024], P(('grp', 'dev'))
- grad_second: float32 [1024, 512], P(('grp', 'dev'))
- new_table: float32 [65536, 128], P('dev')
- new_state: float32 [65536, 128], P('dev')
The draws below stay inside these ranges and needn't reach their ends.
Inputs may be any that keep to these rules, and one draw needn't show every extreme that they name: `block_counts`: the used slots of a block are its first ones. In every draw some owner receives full blocks of 64 used slots from every device. `row_ids`: only used slots are read.
All inputs are finite; a program needn't handle non-finite values.
Results may differ from the reference program's by a relative error of at most 0.0029.
Values may be sent and summed in bfloat16 or wider, within the bound.
No kernel may reach another device: no remote copies, remote signals or barrier semaphores. Data moves between devices by JAX's collectives and lax.ppermute only.
A program may use at most 128 MiB of HBM per device.

```python
import math
import jax
import jax.numpy as jnp
import numpy as np
from jax import lax

IN = 1024
HID = 1024
OUT = 512
E = 128
TROWS_DEV = 2048
CAP = 64
OWNERS = 32
TOKENS = 262144
BLOCKS = 4096
SLOTS = 262144
TABLE_ROWS = 65536


def draw_block_counts(key, part):
    first, second, third = jax.random.split(jax.random.fold_in(key, 11), 3)
    base = jax.random.randint(first, (BLOCKS,), 1, CAP + 1)
    heated = jax.random.randint(second, (OWNERS,), 0, 4) == 0
    forced = jax.random.randint(third, (), 0, OWNERS)
    heated = heated | (jnp.arange(OWNERS) == forced)
    owner = jnp.arange(BLOCKS) % OWNERS
    return jnp.where(heated[owner], CAP, base).astype(jnp.int32)


def place_ends(result, stream_key, least, high):
    place = [jax.random.randint(jax.random.fold_in(stream_key, axis), (), 0, length) for axis, length in enumerate(result.shape)]
    main_axis = result.shape.index(max(result.shape))
    next_to = place[:main_axis] + [(place[main_axis] + 1) % result.shape[main_axis]] + place[main_axis + 1:]
    return result.at[tuple(place)].set(least).at[tuple(next_to)].set(high)


def strengthened(array, own_key, source, target, shards_of, factor):
    def block_of(axis_at):
        return (jnp.arange(array.shape[axis_at]) // (array.shape[axis_at] // shards_of)).reshape((-1,) + (1,) * (array.ndim - 1 - axis_at))

    one_side = jax.random.permutation(own_key, shards_of)[block_of(target)]
    other_side = (block_of(target) + shards_of // 2) % shards_of
    return jnp.where((block_of(source) == one_side) | (block_of(source) == other_side), factor * array, array)


def block_levels(own_key, extent, cuts, least, high):
    loudness, own = 1.0, jax.random.fold_in(own_key, 6)
    for position, parts in cuts:
        steps = jnp.exp(jax.random.uniform(jax.random.fold_in(own, position), (parts,), jnp.float32, least / len(cuts), high / len(cuts)))
        loudness = loudness * jnp.repeat(steps, extent[position] // parts).reshape([-1 if axis == position else 1 for axis in range(len(extent))])
    return loudness


def rank_bounds(amount, skew):
    loads = [(1 << 20) // math.isqrt(standing ** skew) + 1 for standing in range(1, amount + 1)]
    width = 1 + sum(loads) // (1 << 30)
    return np.cumsum(np.array([max(1, weight // width) for weight in loads]))


def ranked_ids(stream_key, extent, amount, skew):
    listing = rank_bounds(amount, skew)
    pick = jax.random.randint(jax.random.fold_in(stream_key, 1), extent, 0, int(listing[amount - 1]))
    rank = jnp.searchsorted(jnp.asarray(listing, jnp.int32), pick, side="right")
    return jax.random.permutation(jax.random.fold_in(stream_key, 2), amount)[rank].astype(jnp.int32)


def centred(key, shape, deviation, bound, cuts=(), held_as=jnp.bfloat16):
    gain = block_levels(key, shape, cuts, -0.22, 0.18) if cuts else 1.0
    values = jax.random.normal(key, shape, jnp.float32) * deviation * gain
    return jnp.minimum(jnp.maximum(values, -bound), bound).astype(held_as)


def noise_with(key, dims, width, reach, pieces, heavy, held_as=jnp.bfloat16):
    drawn = width * jax.random.normal(key, dims, jnp.float32)
    if pieces:
        drawn = drawn * block_levels(key, dims, pieces, -0.22, 0.18)
    return jnp.clip(strengthened(drawn, jax.random.fold_in(key, 3), *heavy), -reach, reach).astype(held_as)


def setup_inputs(seed: int = 0) -> dict:
    streams_of = jax.random.split(jax.random.key(seed), 10)
    return {
        "layer_input": noise_with(streams_of[0], (TOKENS, IN), 1.0, 24.0, ((0, 128),), (0, 1, 128, 5.5)),
        "hidden_pre": noise_with(streams_of[1], (TOKENS, HID), 1.0, 24.0, ((0, 128),), (0, 1, 128, 5.5)),
        "out_grad": centred(streams_of[2], (TOKENS, OUT), 1.0, 6.0, ((0, 128),)),
        "second_weight": centred(streams_of[3], (HID, OUT), OUT ** -0.5, 0.25),
        "row_grads": centred(streams_of[4], (SLOTS, E), 1.0, 6.0, ((0, 128),)),
        "row_ids": place_ends(ranked_ids(streams_of[5], (SLOTS,), TROWS_DEV, 2), jax.random.fold_in(streams_of[5], 3), 0, TROWS_DEV - 1).astype(jnp.int32),
        "block_counts": draw_block_counts(jax.random.fold_in(streams_of[9], 71), 0),
        "emb_table": centred(streams_of[7], (TABLE_ROWS, E), 0.5, 4.0, ((0, 32),), jnp.float32),
        "adagrad_state": jnp.clip(jnp.exp(math.log(1.0) - 4.6051702 * jax.random.uniform(streams_of[8], (TABLE_ROWS, E), jnp.float32) ** block_levels(streams_of[8], (TABLE_ROWS, E), ((0, 32),), -0.2, 0.2)), 0.01, 1.0),
    }


learn_rate = 0.5
epsilon = 1e-08

def reference(layer_input, hidden_pre, out_grad, second_weight, row_grads, row_ids, block_counts, emb_table, adagrad_state):
    active = jnp.maximum(hidden_pre, jnp.zeros_like(hidden_pre))
    back = jnp.dot(out_grad, second_weight.T, preferred_element_type=jnp.float32)
    d_hidden = (back * (hidden_pre > 0).astype(jnp.float32)).astype(jnp.bfloat16)
    contract = (((0,), (0,)), ((), ()))
    grad_first = lax.dot_general(layer_input, d_hidden, contract, preferred_element_type=jnp.float32)
    grad_second = lax.dot_general(active, out_grad, contract, preferred_element_type=jnp.float32)
    slot_index = jnp.arange(row_grads.shape[0], dtype=jnp.int32)
    block_index = slot_index // CAP
    owner = block_index % OWNERS
    usable = slot_index % CAP < block_counts[block_index]
    target = owner * TROWS_DEV + row_ids
    values = row_grads.astype(jnp.float32) * usable.astype(jnp.float32)[:, None]
    table_grad = jax.ops.segment_sum(values, target, num_segments=TABLE_ROWS)
    new_state = adagrad_state + table_grad * table_grad
    new_table = emb_table - learn_rate * table_grad / (jnp.sqrt(new_state) + epsilon)
    return (grad_first, grad_second, new_table, new_state)
```

```python
import jax
import jax.numpy as jnp
from jax import lax
from jax.experimental import pallas as pl
from jax.experimental.pallas import tpu as pltpu
from jax.sharding import Mesh, PartitionSpec as P

learn_rate = 0.5
epsilon = 1e-08
LOW = 64
CHIPS = ("zh", "y", "x", "zl")
DEV = ("y", "x", "zl")
SWAP = ((0, 1), (1, 0))
WIDTH = 256
ROWS_CONTRACTED = (((0,), (0,)), ((), ()))
LANES_CONTRACTED = (((1,), (1,)), ((), ()))
IN_SMEM = pl.BlockSpec(memory_space=pltpu.SMEM)
IN_VMEM = pl.BlockSpec(memory_space=pltpu.VMEM)
IN_HBM = pl.BlockSpec(memory_space=pltpu.HBM)


def in_vmem(array):
    return pltpu.with_memory_space_constraint(array, pltpu.VMEM)


def in_hbm(array):
    return pltpu.with_memory_space_constraint(array, pltpu.HBM)


def pack_kernel(counts_from, ids_from, grads, out, counts, ids, sems):
    blocks, height = out.shape[:2]
    capacity = height - 8
    counts_copy = pltpu.make_async_copy(counts_from, counts, sems.at[0])
    ids_copy = pltpu.make_async_copy(ids_from, ids, sems.at[1])
    grads_copy = pltpu.make_async_copy(grads, out.at[:, pl.ds(0, capacity), :], sems.at[2])
    counts_copy.start()
    ids_copy.start()
    grads_copy.start()
    lane = lax.broadcasted_iota(jnp.int32, (1, 128), 1)
    row = lax.broadcasted_iota(jnp.int32, (8, 128), 0)
    counts_copy.wait()
    ids_copy.wait()
    for block in range(blocks):
        here = ids[pl.ds(block // 2, 1), :]
        turned = pltpu.roll(here, capacity, 1)
        twice = jnp.where((lane < capacity) == (block % 2 == 0), here, turned)
        usable = lax.rem(lane, capacity) < counts[block]
        high = jnp.where(usable, lax.shift_right_logical(twice, 6), 2 * LOW)
        low = jnp.where(usable, lax.bitwise_and(twice, LOW - 1), 0)
        tail = jnp.where(row == 0, high, jnp.where(row == 1, low, 0))
        out[block, pl.ds(capacity, 8), :] = tail.astype(jnp.float32).astype(out.dtype)
    grads_copy.wait()


def packed(counts, ids, grads):
    blocks, width = counts.shape[0], grads.shape[1]
    capacity = grads.shape[0] // blocks
    ids = ids.reshape(-1, 128)
    return pl.pallas_call(
        pack_kernel,
        out_shape=pltpu.VMEM((blocks, capacity + 8, width), grads.dtype),
        in_specs=[IN_HBM] * 3,
        out_specs=IN_VMEM,
        scratch_shapes=[
            pltpu.SMEM((blocks,), jnp.int32),
            pltpu.VMEM(ids.shape, jnp.int32),
            pltpu.SemaphoreType.DMA((3,)),
        ],
        compiler_params=pltpu.CompilerParams(vmem_limit_bytes=8 << 20),
        cost_estimate=pl.CostEstimate(flops=1000000, transcendentals=0, bytes_accessed=1 << 20),
        name="pack_rows",
    )(in_hbm(counts), in_hbm(ids), in_hbm(grads.reshape(blocks, capacity, width)))


def scatter_kernel(core_ref, own, other, out, acc):
    rows = acc.shape[0]
    wanted = core_ref[0] * rows + lax.broadcasted_iota(jnp.int32, (rows, 128), 0)
    lane = lax.broadcasted_iota(jnp.int32, (1, 128), 1)

    def ids_of(blocks, block):
        tail = blocks[block, pl.ds(64, 8), :].astype(jnp.float32)
        return (tail[0:1] * LOW + tail[1:2]).astype(jnp.int32)

    first = True
    for blocks in (own, other):
        for step in range(blocks.shape[0] // 4):
            hot = []
            for block in (4 * step, 4 * step + 2):
                ids = jnp.where(lane < 64, ids_of(blocks, block), ids_of(blocks, block + 1))
                same = wanted == jnp.broadcast_to(ids, (rows, 128))
                hot.append(same.astype(jnp.float32).astype(jnp.bfloat16))
            values = blocks[pl.ds(4 * step, 4), pl.ds(0, 64), :].reshape(256, 128)
            part = jnp.dot(
                jnp.concatenate(hot, axis=1), values, preferred_element_type=jnp.float32
            )
            if first:
                acc[...] = part
                first = False
            else:
                acc[...] += part
    out[...] = acc[...].astype(out.dtype)


def scattered(core, own, other, rows):
    return pl.pallas_call(
        scatter_kernel,
        out_shape=jax.ShapeDtypeStruct((rows, own.shape[2]), jnp.bfloat16),
        in_specs=[IN_SMEM, IN_VMEM, IN_VMEM],
        out_specs=IN_VMEM,
        scratch_shapes=[pltpu.VMEM((rows, own.shape[2]), jnp.float32)],
        compiler_params=pltpu.CompilerParams(vmem_limit_bytes=16 << 20),
        cost_estimate=pl.CostEstimate(flops=1000000000, transcendentals=0, bytes_accessed=1 << 20),
        name="scatter_rows",
    )(core, own, other)


def update_kernel(core_ref, near, far, near_other, far_other, table, state, new_table, new_state):
    half = near.shape[0]

    def apply(place, first, second):
        rows = pl.ds(pl.multiple_of(place * half, half), half)
        grad = first[...].astype(jnp.float32) + second[...].astype(jnp.float32)
        summed = state[rows, :] + grad * grad
        new_state[rows, :] = summed
        new_table[rows, :] = table[rows, :] - learn_rate * grad / (jnp.sqrt(summed) + epsilon)

    apply(core_ref[0], near, far)
    apply(1 - core_ref[0], near_other, far_other)


def updated(core, near, far, near_other, far_other, table, state):
    return pl.pallas_call(
        update_kernel,
        out_shape=(
            jax.ShapeDtypeStruct(table.shape, table.dtype),
            jax.ShapeDtypeStruct(state.shape, state.dtype),
        ),
        in_specs=[IN_SMEM] + [IN_VMEM] * 6,
        out_specs=(IN_VMEM, IN_VMEM),
        compiler_params=pltpu.CompilerParams(vmem_limit_bytes=16 << 20),
        cost_estimate=pl.CostEstimate(flops=2000000, transcendentals=0, bytes_accessed=5 << 20),
        name="update_rows",
    )(core, near, far, near_other, far_other, table, state)


def columns_at(tile, core):
    return pl.ds(pl.multiple_of((2 * tile + core) * WIDTH, WIDTH), WIDTH)


def column_tiles(source, kept, sems, core):
    wanted = [(0, 1 - core), (1, 1 - core), (0, core), (1, core)]
    return [
        pltpu.make_async_copy(
            source.at[:, columns_at(tile, of)],
            kept.at[place],
            sems.at[place],
        )
        for place, (tile, of) in enumerate(wanted)
    ]


def transposed_dot(left, right):
    return lax.dot_general(left, right, ROWS_CONTRACTED, preferred_element_type=jnp.float32)


def active_of(pre):
    return jnp.maximum(pre, jnp.zeros((), pre.dtype))


def theirs_kernel(
    core_ref, grad, weight, hidden, given, d_out, theirs, grad_kept, given_kept, hidden_kept,
    weight_kept, weight_sem, grad_sems, hidden_sems, given_sems,
):
    steps = grad_sems.shape[0]
    height = grad.shape[0] // steps
    core = core_ref[0]
    wide = d_out.shape[1]
    weight_copy = pltpu.make_async_copy(weight, weight_kept, weight_sem)

    def part(source, kept, sems, i):
        rows = pl.ds(i * height, height)
        return pltpu.make_async_copy(source.at[rows, :], kept.at[rows, :], sems.at[i])

    given_copies = column_tiles(given, given_kept, given_sems, core)

    def start_part(i):
        part(grad, grad_kept, grad_sems, i).start()
        part(hidden, hidden_kept, hidden_sems, i).start()

    weight_copy.start()
    start_part(0)
    start_part(1)
    weight_copy.wait()
    for i in range(steps):
        rows = pl.ds(i * height, height)
        part(grad, grad_kept, grad_sems, i).wait()
        part(hidden, hidden_kept, hidden_sems, i).wait()
        if i + 2 < steps:
            start_part(i + 2)
        if steps <= i + 4:
            given_copies[i + 4 - steps].start()
        back = lax.dot_general(
            grad_kept[rows, :], weight_kept[...], LANES_CONTRACTED,
            preferred_element_type=jnp.float32,
        )
        d_out[rows, :] = jnp.where(hidden_kept[rows, :] > 0, back, 0.0).astype(d_out.dtype)

    for place in range(2):
        rows = pl.ds(place * WIDTH, WIDTH)
        given_copies[place].wait()
        theirs[rows, pl.ds(0, wide)] = transposed_dot(given_kept[place], d_out[...]).astype(
            theirs.dtype
        )
    for place in range(2):
        rows = pl.ds(place * WIDTH, WIDTH)
        theirs[rows, pl.ds(wide, grad.shape[1])] = transposed_dot(
            active_of(hidden_kept[:, columns_at(place, 1 - core)]), grad_kept[...]
        ).astype(theirs.dtype)
    for copy in given_copies[2:]:
        copy.wait()


def mine_kernel(core_ref, given_kept, d_hidden, hidden_kept, grad, mine):
    core = core_ref[0]
    wide = d_hidden.shape[1]
    for place in range(2):
        rows = pl.ds(place * WIDTH, WIDTH)
        mine[rows, pl.ds(0, wide)] = transposed_dot(given_kept[2 + place], d_hidden[...])
        mine[rows, pl.ds(wide, grad.shape[1])] = transposed_dot(
            active_of(hidden_kept[:, columns_at(place, core)]), grad[...]
        )


def theirs_of(core, grad, weight, hidden, given):
    tokens, steps = grad.shape[0], 4
    columns = hidden.shape[1] + grad.shape[1]
    return pl.pallas_call(
        theirs_kernel,
        out_shape=(
            pltpu.VMEM(hidden.shape, jnp.bfloat16),
            pltpu.VMEM((2 * WIDTH, columns), jnp.bfloat16),
            pltpu.VMEM(grad.shape, grad.dtype),
            pltpu.VMEM((4, tokens, WIDTH), given.dtype),
            pltpu.VMEM(hidden.shape, hidden.dtype),
        ),
        in_specs=[IN_SMEM] + [IN_HBM] * 4,
        out_specs=(IN_VMEM,) * 5,
        scratch_shapes=[
            pltpu.VMEM(weight.shape, weight.dtype),
            pltpu.SemaphoreType.DMA,
            pltpu.SemaphoreType.DMA((steps,)),
            pltpu.SemaphoreType.DMA((steps,)),
            pltpu.SemaphoreType.DMA((4,)),
        ],
        compiler_params=pltpu.CompilerParams(vmem_limit_bytes=24 << 20),
        cost_estimate=pl.CostEstimate(flops=5400000000, transcendentals=0, bytes_accessed=11 << 20),
        name="theirs_of",
    )(core, in_hbm(grad), in_hbm(weight), in_hbm(hidden), in_hbm(given))


def mine_of(core, given, d_hidden, hidden, grad):
    columns = d_hidden.shape[1] + grad.shape[1]
    return pl.pallas_call(
        mine_kernel,
        out_shape=pltpu.VMEM((2 * WIDTH, columns), jnp.float32),
        in_specs=[IN_SMEM] + [IN_VMEM] * 4,
        out_specs=IN_VMEM,
        compiler_params=pltpu.CompilerParams(vmem_limit_bytes=24 << 20),
        cost_estimate=pl.CostEstimate(flops=3200000000, transcendentals=0, bytes_accessed=2 << 20),
        name="mine_of",
    )(core, in_vmem(given), in_vmem(d_hidden), in_vmem(hidden), in_vmem(grad))


def join_kernel(mine, arrived, out):
    out[...] = (mine[...] + arrived[...].astype(jnp.float32)).astype(out.dtype)


def joined(mine, arrived):
    return pl.pallas_call(
        join_kernel,
        out_shape=pltpu.VMEM(mine.shape, jnp.bfloat16),
        in_specs=[IN_VMEM, IN_VMEM],
        out_specs=IN_VMEM,
        compiler_params=pltpu.CompilerParams(vmem_limit_bytes=16 << 20),
        cost_estimate=pl.CostEstimate(flops=1000000, transcendentals=0, bytes_accessed=2 << 20),
        name="join_halves",
    )(in_vmem(mine), in_vmem(arrived))


def total_kernel(blocks, first, second):
    wide = first.shape[1]
    total = blocks[0].astype(jnp.float32)
    for chip in range(1, blocks.shape[0]):
        total += blocks[chip].astype(jnp.float32)
    first[...] = total[:, :wide]
    second[...] = total[:, wide:]


def totals(blocks, wide):
    rows, columns = blocks.shape[1:]
    return pl.pallas_call(
        total_kernel,
        out_shape=(
            jax.ShapeDtypeStruct((rows, wide), jnp.float32),
            jax.ShapeDtypeStruct((rows, columns - wide), jnp.float32),
        ),
        in_specs=[IN_VMEM],
        out_specs=(IN_VMEM, IN_VMEM),
        compiler_params=pltpu.CompilerParams(vmem_limit_bytes=16 << 20),
        cost_estimate=pl.CostEstimate(flops=1000000, transcendentals=0, bytes_accessed=2 << 20),
        name="total_blocks",
    )(in_vmem(blocks))


def to_owners(share):
    chips = lax.axis_size(CHIPS)
    blocks = share.reshape(chips, share.shape[0] // chips, share.shape[1])
    return lax.all_to_all(blocks, CHIPS, 0, 0, tiled=True)


def on_device(
    layer_input,
    hidden_pre,
    out_grad,
    second_weight,
    row_grads,
    row_ids,
    block_counts,
    emb_table,
    adagrad_state,
):
    at_core = lax.axis_index("c").astype(jnp.int32).reshape(1)
    own = lax.all_to_all(packed(block_counts, row_ids, row_grads), DEV, 0, 0, tiled=True)

    d_hidden, theirs, grad_kept, given_kept, hidden_kept = theirs_of(
        at_core, out_grad, second_weight, hidden_pre, layer_input
    )
    arrived = lax.ppermute(theirs, "c", SWAP)
    mine = mine_of(at_core, given_kept, d_hidden, hidden_kept, grad_kept)
    share = joined(mine, arrived)
    blocks = to_owners(share)
    grad_first, grad_second = totals(blocks, hidden_pre.shape[1])

    other = lax.ppermute(own, "c", SWAP)
    near = scattered(at_core, own, other, emb_table.shape[0] // 2)
    far = lax.ppermute(near, "zh", SWAP)
    near_other = lax.ppermute(near, "c", SWAP)
    far_other = lax.ppermute(far, "c", SWAP)
    new_table, new_state = updated(
        at_core, near, far, near_other, far_other, emb_table, adagrad_state
    )
    return (grad_first, grad_second, new_table, new_state)


def solution(mesh):
    names = ("zh", "c", "y", "x", "zl")
    split = Mesh(mesh.devices.reshape(2, 2, 4, 4, 2), names)
    every = P(names, None)
    in_specs = (
        every,
        every,
        every,
        P(),
        every,
        P(names),
        P(names),
        P(DEV, None),
        P(DEV, None),
    )
    out_specs = (every, every, P(DEV, None), P(DEV, None))
    return jax.shard_map(
        on_device, mesh=split, in_specs=in_specs, out_specs=out_specs, check_vma=False
    )
```

```python
import jax
import jax.numpy as jnp
from jax import lax
from jax.experimental import pallas as pl
from jax.experimental.pallas import tpu as pltpu
from jax.sharding import Mesh, PartitionSpec as P

learn_rate = 0.5
epsilon = 1e-08
LOW = 64
CHIPS = ("zh", "y", "x", "zl")
DEV = ("y", "x", "zl")
SWAP = ((0, 1), (1, 0))
WIDTH = 256
ROWS_CONTRACTED = (((0,), (0,)), ((), ()))
LANES_CONTRACTED = (((1,), (1,)), ((), ()))
IN_SMEM = pl.BlockSpec(memory_space=pltpu.SMEM)
IN_VMEM = pl.BlockSpec(memory_space=pltpu.VMEM)
IN_HBM = pl.BlockSpec(memory_space=pltpu.HBM)


def in_vmem(array):
    return pltpu.with_memory_space_constraint(array, pltpu.VMEM)


def in_hbm(array):
    return pltpu.with_memory_space_constraint(array, pltpu.HBM)


def pack_kernel(counts_from, ids_from, grads, out, counts, ids, sems):
    blocks, height = out.shape[:2]
    capacity = height - 8
    counts_copy = pltpu.make_async_copy(counts_from, counts, sems.at[0])
    ids_copy = pltpu.make_async_copy(ids_from, ids, sems.at[1])
    grads_copy = pltpu.make_async_copy(grads, out.at[:, pl.ds(0, capacity), :], sems.at[2])
    counts_copy.start()
    ids_copy.start()
    grads_copy.start()
    lane = lax.broadcasted_iota(jnp.int32, (1, 128), 1)
    row = lax.broadcasted_iota(jnp.int32, (8, 128), 0)
    counts_copy.wait()
    ids_copy.wait()
    for block in range(blocks):
        here = ids[pl.ds(block // 2, 1), :]
        turned = pltpu.roll(here, capacity, 1)
        twice = jnp.where((lane < capacity) == (block % 2 == 0), here, turned)
        usable = lax.rem(lane, capacity) < counts[block]
        high = jnp.where(usable, lax.shift_right_logical(twice, 6), 2 * LOW)
        low = jnp.where(usable, lax.bitwise_and(twice, LOW - 1), 0)
        tail = jnp.where(row == 0, high, jnp.where(row == 1, low, 0))
        out[block, pl.ds(capacity, 8), :] = tail.astype(jnp.float32).astype(out.dtype)
    grads_copy.wait()


def packed(counts, ids, grads):
    blocks, width = counts.shape[0], grads.shape[1]
    capacity = grads.shape[0] // blocks
    ids = ids.reshape(-1, 128)
    return pl.pallas_call(
        pack_kernel,
        out_shape=pltpu.VMEM((blocks, capacity + 8, width), grads.dtype),
        in_specs=[IN_HBM] * 3,
        out_specs=IN_VMEM,
        scratch_shapes=[
            pltpu.SMEM((blocks,), jnp.int32),
            pltpu.VMEM(ids.shape, jnp.int32),
            pltpu.SemaphoreType.DMA((3,)),
        ],
        compiler_params=pltpu.CompilerParams(vmem_limit_bytes=8 << 20),
        cost_estimate=pl.CostEstimate(flops=1000000, transcendentals=0, bytes_accessed=1 << 20),
        name="pack_rows",
    )(in_hbm(counts), in_hbm(ids), in_hbm(grads.reshape(blocks, capacity, width)))


def scatter_kernel(core_ref, own, other, out, acc):
    rows = acc.shape[0]
    wanted = core_ref[0] * rows + lax.broadcasted_iota(jnp.int32, (rows, 128), 0)
    lane = lax.broadcasted_iota(jnp.int32, (1, 128), 1)

    def ids_of(blocks, block):
        tail = blocks[block, pl.ds(64, 8), :].astype(jnp.float32)
        return (tail[0:1] * LOW + tail[1:2]).astype(jnp.int32)

    first = True
    for blocks in (own, other):
        for step in range(blocks.shape[0] // 4):
            hot = []
            for block in (4 * step, 4 * step + 2):
                ids = jnp.where(lane < 64, ids_of(blocks, block), ids_of(blocks, block + 1))
                same = wanted == jnp.broadcast_to(ids, (rows, 128))
                hot.append(same.astype(jnp.float32).astype(jnp.bfloat16))
            values = blocks[pl.ds(4 * step, 4), pl.ds(0, 64), :].reshape(256, 128)
            part = jnp.dot(
                jnp.concatenate(hot, axis=1), values, preferred_element_type=jnp.float32
            )
            if first:
                acc[...] = part
                first = False
            else:
                acc[...] += part
    out[...] = acc[...].astype(out.dtype)


def scattered(core, own, other, rows):
    return pl.pallas_call(
        scatter_kernel,
        out_shape=pltpu.VMEM((rows, own.shape[2]), jnp.float32),
        in_specs=[IN_SMEM, IN_VMEM, IN_VMEM],
        out_specs=IN_VMEM,
        scratch_shapes=[pltpu.VMEM((rows, own.shape[2]), jnp.float32)],
        compiler_params=pltpu.CompilerParams(vmem_limit_bytes=16 << 20),
        cost_estimate=pl.CostEstimate(flops=1000000000, transcendentals=0, bytes_accessed=1 << 20),
        name="scatter_rows",
    )(core, in_vmem(own), in_vmem(other))


def update_kernel(core_ref, total, total_other, table, state, new_table, new_state):
    half = total.shape[0]

    def apply(place, grads):
        rows = pl.ds(pl.multiple_of(place * half, half), half)
        grad = grads[...]
        summed = state[rows, :] + grad * grad
        new_state[rows, :] = summed
        new_table[rows, :] = table[rows, :] - learn_rate * grad / (jnp.sqrt(summed) + epsilon)

    apply(core_ref[0], total)
    apply(1 - core_ref[0], total_other)


def updated(core, total, total_other, table, state):
    return pl.pallas_call(
        update_kernel,
        out_shape=(
            jax.ShapeDtypeStruct(table.shape, table.dtype),
            jax.ShapeDtypeStruct(state.shape, state.dtype),
        ),
        in_specs=[IN_SMEM] + [IN_VMEM] * 4,
        out_specs=(IN_VMEM, IN_VMEM),
        compiler_params=pltpu.CompilerParams(vmem_limit_bytes=16 << 20),
        cost_estimate=pl.CostEstimate(flops=2000000, transcendentals=0, bytes_accessed=5 << 20),
        name="update_rows",
    )(core, total, total_other, table, state)


def columns_at(tile, core):
    return pl.ds(pl.multiple_of((2 * tile + core) * WIDTH, WIDTH), WIDTH)


def column_tiles(source, kept, sems, core):
    wanted = [(0, 1 - core), (1, 1 - core), (0, core), (1, core)]
    return [
        pltpu.make_async_copy(
            source.at[:, columns_at(tile, of)],
            kept.at[place],
            sems.at[place],
        )
        for place, (tile, of) in enumerate(wanted)
    ]


def transposed_dot(left, right):
    return lax.dot_general(left, right, ROWS_CONTRACTED, preferred_element_type=jnp.float32)


def active_of(pre):
    return jnp.maximum(pre, jnp.zeros((), pre.dtype))


def theirs_kernel(
    core_ref, grad, weight, hidden, given, d_out, theirs, grad_kept, given_kept, hidden_kept,
    weight_kept, weight_sem, grad_sems, hidden_sems, given_sems,
):
    steps = grad_sems.shape[0]
    height = grad.shape[0] // steps
    core = core_ref[0]
    wide = d_out.shape[1]
    weight_copy = pltpu.make_async_copy(weight, weight_kept, weight_sem)

    def part(source, kept, sems, i):
        rows = pl.ds(i * height, height)
        return pltpu.make_async_copy(source.at[rows, :], kept.at[rows, :], sems.at[i])

    given_copies = column_tiles(given, given_kept, given_sems, core)

    def start_part(i):
        part(grad, grad_kept, grad_sems, i).start()
        part(hidden, hidden_kept, hidden_sems, i).start()

    weight_copy.start()
    start_part(0)
    start_part(1)
    weight_copy.wait()
    for i in range(steps):
        rows = pl.ds(i * height, height)
        part(grad, grad_kept, grad_sems, i).wait()
        part(hidden, hidden_kept, hidden_sems, i).wait()
        if i + 2 < steps:
            start_part(i + 2)
        if steps <= i + 4:
            given_copies[i + 4 - steps].start()
        back = lax.dot_general(
            grad_kept[rows, :], weight_kept[...], LANES_CONTRACTED,
            preferred_element_type=jnp.float32,
        )
        d_out[rows, :] = jnp.where(hidden_kept[rows, :] > 0, back, 0.0).astype(d_out.dtype)

    for place in range(2):
        rows = pl.ds(place * WIDTH, WIDTH)
        given_copies[place].wait()
        theirs[rows, pl.ds(0, wide)] = transposed_dot(given_kept[place], d_out[...]).astype(
            theirs.dtype
        )
    for place in range(2):
        rows = pl.ds(place * WIDTH, WIDTH)
        theirs[rows, pl.ds(wide, grad.shape[1])] = transposed_dot(
            active_of(hidden_kept[:, columns_at(place, 1 - core)]), grad_kept[...]
        ).astype(theirs.dtype)
    for copy in given_copies[2:]:
        copy.wait()


def mine_kernel(core_ref, given_kept, d_hidden, hidden_kept, grad, mine):
    core = core_ref[0]
    wide = d_hidden.shape[1]
    for place in range(2):
        rows = pl.ds(place * WIDTH, WIDTH)
        mine[rows, pl.ds(0, wide)] = transposed_dot(given_kept[2 + place], d_hidden[...])
        mine[rows, pl.ds(wide, grad.shape[1])] = transposed_dot(
            active_of(hidden_kept[:, columns_at(place, core)]), grad[...]
        )


def theirs_of(core, grad, weight, hidden, given):
    tokens, steps = grad.shape[0], 4
    columns = hidden.shape[1] + grad.shape[1]
    return pl.pallas_call(
        theirs_kernel,
        out_shape=(
            pltpu.VMEM(hidden.shape, jnp.bfloat16),
            pltpu.VMEM((2 * WIDTH, columns), jnp.bfloat16),
            pltpu.VMEM(grad.shape, grad.dtype),
            pltpu.VMEM((4, tokens, WIDTH), given.dtype),
            pltpu.VMEM(hidden.shape, hidden.dtype),
        ),
        in_specs=[IN_SMEM] + [IN_HBM] * 4,
        out_specs=(IN_VMEM,) * 5,
        scratch_shapes=[
            pltpu.VMEM(weight.shape, weight.dtype),
            pltpu.SemaphoreType.DMA,
            pltpu.SemaphoreType.DMA((steps,)),
            pltpu.SemaphoreType.DMA((steps,)),
            pltpu.SemaphoreType.DMA((4,)),
        ],
        compiler_params=pltpu.CompilerParams(vmem_limit_bytes=24 << 20),
        cost_estimate=pl.CostEstimate(flops=5400000000, transcendentals=0, bytes_accessed=11 << 20),
        name="theirs_of",
    )(core, in_hbm(grad), in_hbm(weight), in_hbm(hidden), in_hbm(given))


def mine_of(core, given, d_hidden, hidden, grad):
    columns = d_hidden.shape[1] + grad.shape[1]
    return pl.pallas_call(
        mine_kernel,
        out_shape=pltpu.VMEM((2 * WIDTH, columns), jnp.float32),
        in_specs=[IN_SMEM] + [IN_VMEM] * 4,
        out_specs=IN_VMEM,
        compiler_params=pltpu.CompilerParams(vmem_limit_bytes=24 << 20),
        cost_estimate=pl.CostEstimate(flops=3200000000, transcendentals=0, bytes_accessed=2 << 20),
        name="mine_of",
    )(core, in_vmem(given), in_vmem(d_hidden), in_vmem(hidden), in_vmem(grad))


def join_kernel(mine, arrived, out):
    out[...] = (mine[...] + arrived[...].astype(jnp.float32)).astype(out.dtype)


def joined(mine, arrived):
    return pl.pallas_call(
        join_kernel,
        out_shape=pltpu.VMEM(mine.shape, jnp.bfloat16),
        in_specs=[IN_VMEM, IN_VMEM],
        out_specs=IN_VMEM,
        compiler_params=pltpu.CompilerParams(vmem_limit_bytes=16 << 20),
        cost_estimate=pl.CostEstimate(flops=1000000, transcendentals=0, bytes_accessed=2 << 20),
        name="join_halves",
    )(in_vmem(mine), in_vmem(arrived))


def total_kernel(blocks, first, second):
    wide = first.shape[1]
    total = blocks[0].astype(jnp.float32)
    for chip in range(1, blocks.shape[0]):
        total += blocks[chip].astype(jnp.float32)
    first[...] = total[:, :wide]
    second[...] = total[:, wide:]


def totals(blocks, wide):
    rows, columns = blocks.shape[1:]
    return pl.pallas_call(
        total_kernel,
        out_shape=(
            jax.ShapeDtypeStruct((rows, wide), jnp.float32),
            jax.ShapeDtypeStruct((rows, columns - wide), jnp.float32),
        ),
        in_specs=[IN_VMEM],
        out_specs=(IN_VMEM, IN_VMEM),
        compiler_params=pltpu.CompilerParams(vmem_limit_bytes=16 << 20),
        cost_estimate=pl.CostEstimate(flops=1000000, transcendentals=0, bytes_accessed=2 << 20),
        name="total_blocks",
    )(in_vmem(blocks))


def to_owners(share):
    chips = lax.axis_size(CHIPS)
    blocks = share.reshape(chips, share.shape[0] // chips, share.shape[1])
    return lax.all_to_all(blocks, CHIPS, 0, 0, tiled=True)


def on_device(
    layer_input,
    hidden_pre,
    out_grad,
    second_weight,
    row_grads,
    row_ids,
    block_counts,
    emb_table,
    adagrad_state,
):
    at_core = lax.axis_index("c").astype(jnp.int32).reshape(1)
    own = lax.all_to_all(packed(block_counts, row_ids, row_grads), DEV, 0, 0, tiled=True)

    d_hidden, theirs, grad_kept, given_kept, hidden_kept = theirs_of(
        at_core, out_grad, second_weight, hidden_pre, layer_input
    )
    arrived = lax.ppermute(theirs, "c", SWAP)
    mine = mine_of(at_core, given_kept, d_hidden, hidden_kept, grad_kept)
    share = joined(mine, arrived)
    blocks = to_owners(share)
    grad_first, grad_second = totals(blocks, hidden_pre.shape[1])

    other = lax.ppermute(own, "c", SWAP)
    near = scattered(at_core, own, other, emb_table.shape[0] // 2)
    near = lax.optimization_barrier(near.astype(jnp.float16))
    far = lax.ppermute(near, "zh", SWAP)
    total = near.astype(jnp.float32) + far.astype(jnp.float32)
    total_other = lax.ppermute(total, "c", SWAP)
    new_table, new_state = updated(at_core, total, total_other, emb_table, adagrad_state)
    return (grad_first, grad_second, new_table, new_state)


def solution(mesh):
    names = ("zh", "c", "y", "x", "zl")
    split = Mesh(mesh.devices.reshape(2, 2, 4, 4, 2), names)
    every = P(names, None)
    in_specs = (
        every,
        every,
        every,
        P(),
        every,
        P(names),
        P(names),
        P(DEV, None),
        P(DEV, None),
    )
    out_specs = (every, every, P(DEV, None), P(DEV, None))
    return jax.shard_map(
        on_device, mesh=split, in_specs=in_specs, out_specs=out_specs, check_vma=False
    )
```

```python
import jax
import jax.numpy as jnp
from jax import lax
from jax.experimental import pallas as pl
from jax.experimental.pallas import tpu as pltpu
from jax.sharding import Mesh, PartitionSpec as P

learn_rate = 0.5
epsilon = 1e-08
LOW = 64
CHIPS = ("zh", "y", "x", "zl")
DEV = ("y", "x", "zl")
SWAP = ((0, 1), (1, 0))
WIDTH = 256
ROWS_CONTRACTED = (((0,), (0,)), ((), ()))
LANES_CONTRACTED = (((1,), (1,)), ((), ()))
IN_SMEM = pl.BlockSpec(memory_space=pltpu.SMEM)
IN_VMEM = pl.BlockSpec(memory_space=pltpu.VMEM)
IN_HBM = pl.BlockSpec(memory_space=pltpu.HBM)


def in_vmem(array):
    return pltpu.with_memory_space_constraint(array, pltpu.VMEM)


def in_hbm(array):
    return pltpu.with_memory_space_constraint(array, pltpu.HBM)


def pack_kernel(counts_from, ids_from, grads, out, counts, ids, kept, tails, sems):
    blocks, height = out.shape[:2]
    capacity = height - 8
    counts_copy = pltpu.make_async_copy(counts_from, counts, sems.at[0])
    ids_copy = pltpu.make_async_copy(ids_from, ids, sems.at[1])
    grads_copy = pltpu.make_async_copy(grads, kept, sems.at[2])
    grads_out = pltpu.make_async_copy(kept, out.at[:, pl.ds(0, capacity), :], sems.at[3])
    tails_out = pltpu.make_async_copy(tails, out.at[:, pl.ds(capacity, 8), :], sems.at[4])
    copy_all([counts_copy, ids_copy, grads_copy])
    lane = lax.broadcasted_iota(jnp.int32, (1, 128), 1)
    row = lax.broadcasted_iota(jnp.int32, (8, 128), 0)
    grads_copy.wait()
    grads_out.start()
    counts_copy.wait()
    ids_copy.wait()
    here = ids[...]
    turned = pltpu.roll(here, capacity, 1)
    for block in range(blocks):
        pair = block // 2
        left = lane < capacity
        twice = jnp.where(
            left == (block % 2 == 0), here[pair : pair + 1], turned[pair : pair + 1]
        )
        usable = lax.rem(lane, capacity) < counts[block]
        high = jnp.where(usable, lax.shift_right_logical(twice, 6), 2 * LOW)
        low = jnp.where(usable, lax.bitwise_and(twice, LOW - 1), 0)
        tail = jnp.where(row == 0, high, jnp.where(row == 1, low, 0))
        tails[block] = tail.astype(jnp.float32).astype(out.dtype)
    tails_out.start()
    grads_out.wait()
    tails_out.wait()


def packed(counts, ids, grads):
    blocks, width = counts.shape[0], grads.shape[1]
    capacity = grads.shape[0] // blocks
    ids = ids.reshape(-1, 128)
    return pl.pallas_call(
        pack_kernel,
        out_shape=pltpu.HBM((blocks, capacity + 8, width), grads.dtype),
        in_specs=[IN_HBM] * 3,
        out_specs=IN_HBM,
        scratch_shapes=[
            pltpu.SMEM((blocks,), jnp.int32),
            pltpu.VMEM(ids.shape, jnp.int32),
            pltpu.VMEM((blocks, capacity, width), grads.dtype),
            pltpu.VMEM((blocks, 8, width), grads.dtype),
            pltpu.SemaphoreType.DMA((5,)),
        ],
        compiler_params=pltpu.CompilerParams(vmem_limit_bytes=8 << 20),
        cost_estimate=pl.CostEstimate(flops=1000000, transcendentals=0, bytes_accessed=1 << 20),
        name="pack_rows",
    )(in_hbm(counts), in_hbm(ids), in_hbm(grads.reshape(blocks, capacity, width)))


def scatter_into(core_ref, blocks, acc, out):
    rows = out.shape[0]
    wanted = core_ref[0] * rows + lax.broadcasted_iota(jnp.int32, (rows, 128), 0)
    lane = lax.broadcasted_iota(jnp.int32, (1, 128), 1)

    def ids_of(block):
        tail = blocks[block, pl.ds(64, 8), :].astype(jnp.float32)
        return (tail[0:1] * LOW + tail[1:2]).astype(jnp.int32)

    total = None if acc is None else acc[...]
    for step in range(blocks.shape[0] // 4):
        hot = []
        for block in (4 * step, 4 * step + 2):
            ids = jnp.where(lane < 64, ids_of(block), ids_of(block + 1))
            same = wanted == jnp.broadcast_to(ids, (rows, 128))
            hot.append(same.astype(jnp.float32).astype(jnp.bfloat16))
        values = blocks[pl.ds(4 * step, 4), pl.ds(0, 64), :].reshape(256, 128)
        part = jnp.dot(jnp.concatenate(hot, axis=1), values, preferred_element_type=jnp.float32)
        out[...] = part if total is None else total + part
        total = out[...]


def scatter_own_kernel(core_ref, blocks, out):
    scatter_into(core_ref, blocks, None, out)


def scatter_other_kernel(core_ref, blocks, acc, out):
    scatter_into(core_ref, blocks, acc, out)


def scattered(kernel, core, rows, blocks, *acc):
    return pl.pallas_call(
        kernel,
        out_shape=pltpu.VMEM((rows, blocks.shape[2]), jnp.float32),
        in_specs=[IN_SMEM] + [IN_VMEM] * (1 + len(acc)),
        out_specs=IN_VMEM,
        compiler_params=pltpu.CompilerParams(vmem_limit_bytes=16 << 20),
        cost_estimate=pl.CostEstimate(flops=500000000, transcendentals=0, bytes_accessed=1 << 20),
    )(core, in_vmem(blocks), *acc)


def update_kernel(core_ref, total, total_other, table, state, new_table, new_state, kept, sems):
    half = total.shape[0]
    copies = []
    for i, source in enumerate((table, state)):
        for part in range(2):
            rows = pl.ds(part * half, half)
            copies.append(
                pltpu.make_async_copy(source.at[rows, :], kept.at[i, rows, :], sems.at[i, part])
            )
    copy_all(copies)
    for copy in copies:
        copy.wait()

    def apply(place, grads):
        rows = pl.ds(pl.multiple_of(place * half, half), half)
        grad = grads[...]
        summed = kept[1, rows, :] + grad * grad
        new_state[rows, :] = summed
        new_table[rows, :] = kept[0, rows, :] - learn_rate * grad / (jnp.sqrt(summed) + epsilon)

    apply(core_ref[0], total)
    apply(1 - core_ref[0], total_other)


def updated(core, total, total_other, table, state):
    return pl.pallas_call(
        update_kernel,
        out_shape=(
            jax.ShapeDtypeStruct(table.shape, table.dtype),
            jax.ShapeDtypeStruct(state.shape, state.dtype),
        ),
        in_specs=[IN_SMEM, IN_VMEM, IN_VMEM, IN_HBM, IN_HBM],
        out_specs=(IN_VMEM, IN_VMEM),
        scratch_shapes=[
            pltpu.VMEM((2,) + table.shape, table.dtype),
            pltpu.SemaphoreType.DMA((2, 2)),
        ],
        compiler_params=pltpu.CompilerParams(vmem_limit_bytes=16 << 20),
        cost_estimate=pl.CostEstimate(flops=2000000, transcendentals=0, bytes_accessed=5 << 20),
        name="update_rows",
    )(core, total, total_other, in_hbm(table), in_hbm(state))


def copy_all(copies):
    for copy in copies:
        copy.start()


def columns_at(tile, core):
    return pl.ds(pl.multiple_of((2 * tile + core) * WIDTH, WIDTH), WIDTH)


def column_tiles(source, kept, sems, core):
    wanted = [(0, 1 - core), (1, 1 - core), (0, core), (1, core)]
    return [
        pltpu.make_async_copy(
            source.at[:, columns_at(tile, of)],
            kept.at[place // 2, :, pl.ds(place % 2 * WIDTH, WIDTH)],
            sems.at[place],
        )
        for place, (tile, of) in enumerate(wanted)
    ]


def transposed_dot(left, right):
    return lax.dot_general(left, right, ROWS_CONTRACTED, preferred_element_type=jnp.float32)


def active_of(hidden, core):
    pre = jnp.concatenate([hidden[:, columns_at(tile, core)] for tile in range(2)], axis=1)
    return jnp.maximum(pre, jnp.zeros((), pre.dtype))


def theirs_kernel(
    core_ref, grad, weight, hidden, given, d_out, theirs, grad_kept, given_kept, hidden_kept,
    weight_kept, weight_sem, grad_sems, hidden_sems, given_sems,
):
    steps = grad_sems.shape[0]
    unit = grad.shape[0] // 8
    begins = (0, 2, 4, 6, 8)
    core = core_ref[0]
    wide = d_out.shape[1]
    weight_copy = pltpu.make_async_copy(weight, weight_kept, weight_sem)

    def part(source, kept, sems, i):
        rows = pl.ds(begins[i] * unit, (begins[i + 1] - begins[i]) * unit)
        return pltpu.make_async_copy(source.at[rows, :], kept.at[rows, :], sems.at[i])

    given_copies = column_tiles(given, given_kept, given_sems, core)

    def start_part(i):
        part(grad, grad_kept, grad_sems, i).start()
        part(hidden, hidden_kept, hidden_sems, i).start()

    weight_copy.start()
    start_part(0)
    start_part(1)
    weight_copy.wait()
    for i in range(steps):
        rows = pl.ds(begins[i] * unit, (begins[i + 1] - begins[i]) * unit)
        part(grad, grad_kept, grad_sems, i).wait()
        part(hidden, hidden_kept, hidden_sems, i).wait()
        if i + 2 < steps:
            start_part(i + 2)
        if steps <= i + 4:
            given_copies[i + 4 - steps].start()
        back = lax.dot_general(
            grad_kept[rows, :], weight_kept[...], LANES_CONTRACTED,
            preferred_element_type=jnp.float32,
        )
        d_out[rows, :] = jnp.where(hidden_kept[rows, :] > 0, back, 0.0).astype(d_out.dtype)

    given_copies[0].wait()
    given_copies[1].wait()
    theirs[:, pl.ds(0, wide)] = transposed_dot(given_kept[0], d_out[...]).astype(theirs.dtype)
    theirs[:, pl.ds(wide, grad.shape[1])] = transposed_dot(
        active_of(hidden_kept, 1 - core), grad_kept[...]
    ).astype(theirs.dtype)
    for copy in given_copies[2:]:
        copy.wait()


def mine_kernel(core_ref, given_kept, d_hidden, hidden_kept, grad, mine):
    wide = d_hidden.shape[1]
    mine[:, pl.ds(0, wide)] = transposed_dot(given_kept[1], d_hidden[...])
    mine[:, pl.ds(wide, grad.shape[1])] = transposed_dot(
        active_of(hidden_kept, core_ref[0]), grad[...]
    )


def theirs_of(core, grad, weight, hidden, given):
    tokens, steps = grad.shape[0], 4
    columns = hidden.shape[1] + grad.shape[1]
    return pl.pallas_call(
        theirs_kernel,
        out_shape=(
            pltpu.VMEM(hidden.shape, jnp.bfloat16),
            pltpu.VMEM((2 * WIDTH, columns), jnp.bfloat16),
            pltpu.VMEM(grad.shape, grad.dtype),
            pltpu.VMEM((2, tokens, 2 * WIDTH), given.dtype),
            pltpu.VMEM(hidden.shape, hidden.dtype),
        ),
        in_specs=[IN_SMEM] + [IN_HBM] * 4,
        out_specs=(IN_VMEM,) * 5,
        scratch_shapes=[
            pltpu.VMEM(weight.shape, weight.dtype),
            pltpu.SemaphoreType.DMA,
            pltpu.SemaphoreType.DMA((steps,)),
            pltpu.SemaphoreType.DMA((steps,)),
            pltpu.SemaphoreType.DMA((4,)),
        ],
        compiler_params=pltpu.CompilerParams(vmem_limit_bytes=24 << 20),
        cost_estimate=pl.CostEstimate(flops=5400000000, transcendentals=0, bytes_accessed=11 << 20),
        name="theirs_of",
    )(core, in_hbm(grad), in_hbm(weight), in_hbm(hidden), in_hbm(given))


def mine_of(core, given, d_hidden, hidden, grad):
    columns = d_hidden.shape[1] + grad.shape[1]
    return pl.pallas_call(
        mine_kernel,
        out_shape=pltpu.VMEM((2 * WIDTH, columns), jnp.float32),
        in_specs=[IN_SMEM] + [IN_VMEM] * 4,
        out_specs=IN_VMEM,
        compiler_params=pltpu.CompilerParams(vmem_limit_bytes=24 << 20),
        cost_estimate=pl.CostEstimate(flops=3200000000, transcendentals=0, bytes_accessed=2 << 20),
        name="mine_of",
    )(core, in_vmem(given), in_vmem(d_hidden), in_vmem(hidden), in_vmem(grad))


def join_kernel(mine, arrived, out, kept, sems):
    parts = sems.shape[0]
    height = mine.shape[0] // parts
    copies = []
    for part in range(parts):
        rows = pl.ds(part * height, height)
        kept[rows, :] = (mine[rows, :] + arrived[rows, :].astype(jnp.float32)).astype(kept.dtype)
        copies.append(pltpu.make_async_copy(kept.at[rows, :], out.at[rows, :], sems.at[part]))
        copies[-1].start()
    for copy in copies:
        copy.wait()


def joined(mine, arrived):
    return pl.pallas_call(
        join_kernel,
        out_shape=pltpu.HBM(mine.shape, jnp.bfloat16),
        in_specs=[IN_VMEM, IN_VMEM],
        out_specs=IN_HBM,
        scratch_shapes=[pltpu.VMEM(mine.shape, jnp.bfloat16), pltpu.SemaphoreType.DMA((4,))],
        compiler_params=pltpu.CompilerParams(vmem_limit_bytes=16 << 20),
        cost_estimate=pl.CostEstimate(flops=1000000, transcendentals=0, bytes_accessed=2 << 20),
        name="join_halves",
    )(in_vmem(mine), in_vmem(arrived))


def total_kernel(blocks, first, second):
    wide = first.shape[1]
    total = blocks[0].astype(jnp.float32)
    for chip in range(1, blocks.shape[0]):
        total += blocks[chip].astype(jnp.float32)
    first[...] = total[:, :wide]
    second[...] = total[:, wide:]


def totals(blocks, wide):
    rows, columns = blocks.shape[1:]
    return pl.pallas_call(
        total_kernel,
        out_shape=(
            jax.ShapeDtypeStruct((rows, wide), jnp.float32),
            jax.ShapeDtypeStruct((rows, columns - wide), jnp.float32),
        ),
        in_specs=[IN_VMEM],
        out_specs=(IN_VMEM, IN_VMEM),
        compiler_params=pltpu.CompilerParams(vmem_limit_bytes=16 << 20),
        cost_estimate=pl.CostEstimate(flops=1000000, transcendentals=0, bytes_accessed=2 << 20),
        name="total_blocks",
    )(in_vmem(blocks))


def to_owners(share):
    chips = lax.axis_size(CHIPS)
    blocks = share.reshape(chips, share.shape[0] // chips, share.shape[1])
    return lax.all_to_all(blocks, CHIPS, 0, 0, tiled=True)


def on_device(
    layer_input,
    hidden_pre,
    out_grad,
    second_weight,
    row_grads,
    row_ids,
    block_counts,
    emb_table,
    adagrad_state,
):
    at_core = lax.axis_index("c").astype(jnp.int32).reshape(1)
    message = packed(block_counts, row_ids, row_grads)
    own = lax.all_to_all(message, DEV, 0, 0, tiled=True)

    d_hidden, theirs, grad_kept, given_kept, hidden_kept = theirs_of(
        at_core, out_grad, second_weight, hidden_pre, layer_input
    )
    arrived = lax.ppermute(theirs, "c", SWAP)
    mine = mine_of(at_core, given_kept, d_hidden, hidden_kept, grad_kept)
    share = joined(mine, arrived)
    blocks = to_owners(share)
    grad_first, grad_second = totals(blocks, hidden_pre.shape[1])

    other = lax.ppermute(own, "c", SWAP)
    half = emb_table.shape[0] // 2
    near = scattered(scatter_own_kernel, at_core, half, own)
    near = scattered(scatter_other_kernel, at_core, half, other, near)
    near = lax.optimization_barrier(near.astype(jnp.float16))
    far = lax.ppermute(near, "zh", SWAP)
    total = near.astype(jnp.float32) + far.astype(jnp.float32)
    total_other = lax.ppermute(total, "c", SWAP)
    new_table, new_state = updated(at_core, total, total_other, emb_table, adagrad_state)
    return (grad_first, grad_second, new_table, new_state)


def solution(mesh):
    names = ("zh", "c", "y", "x", "zl")
    split = Mesh(mesh.devices.reshape(2, 2, 4, 4, 2), names)
    every = P(names, None)
    in_specs = (
        every,
        every,
        every,
        P(),
        every,
        P(names),
        P(names),
        P(DEV, None),
        P(DEV, None),
    )
    out_specs = (every, every, P(DEV, None), P(DEV, None))
    return jax.shard_map(
        on_device, mesh=split, in_specs=in_specs, out_specs=out_specs, check_vma=False
    )
```

```python
import jax
import jax.numpy as jnp
from jax import lax
from jax.experimental import pallas as pl
from jax.experimental.pallas import tpu as pltpu
from jax.sharding import Mesh, PartitionSpec as P

learn_rate = 0.5
epsilon = 1e-08
LOW = 64
CHIPS = ("zh", "y", "x", "zl")
DEV = ("y", "x", "zl")
SWAP = ((0, 1), (1, 0))
WIDTH = 256
ROWS_CONTRACTED = (((0,), (0,)), ((), ()))
LANES_CONTRACTED = (((1,), (1,)), ((), ()))
IN_SMEM = pl.BlockSpec(memory_space=pltpu.SMEM)
IN_VMEM = pl.BlockSpec(memory_space=pltpu.VMEM)
IN_HBM = pl.BlockSpec(memory_space=pltpu.HBM)


def in_vmem(array):
    return pltpu.with_memory_space_constraint(array, pltpu.VMEM)


def in_hbm(array):
    return pltpu.with_memory_space_constraint(array, pltpu.HBM)


def pack_kernel(
    counts_from, ids_from, grads, weight, grad, hidden, out, weight_kept, grad_head, hidden_head,
    counts, ids, kept, tails, sems,
):
    blocks, height = out.shape[:2]
    capacity = height - 8
    counts_copy = pltpu.make_async_copy(counts_from, counts, sems.at[0])
    ids_copy = pltpu.make_async_copy(ids_from, ids, sems.at[1])
    grads_copy = pltpu.make_async_copy(grads, kept, sems.at[2])
    grads_out = pltpu.make_async_copy(kept, out.at[:, pl.ds(0, capacity), :], sems.at[3])
    tails_out = pltpu.make_async_copy(tails, out.at[:, pl.ds(capacity, 8), :], sems.at[4])
    head = pl.ds(0, grad_head.shape[0])
    heads = [
        pltpu.make_async_copy(weight, weight_kept, sems.at[5]),
        pltpu.make_async_copy(grad.at[head, :], grad_head, sems.at[6]),
        pltpu.make_async_copy(hidden.at[head, :], hidden_head, sems.at[7]),
    ]
    copy_all([counts_copy, ids_copy, grads_copy] + heads)
    lane = lax.broadcasted_iota(jnp.int32, (1, 128), 1)
    row = lax.broadcasted_iota(jnp.int32, (8, 128), 0)
    grads_copy.wait()
    grads_out.start()
    counts_copy.wait()
    ids_copy.wait()
    here = ids[...]
    turned = pltpu.roll(here, capacity, 1)
    for block in range(blocks):
        pair = block // 2
        left = lane < capacity
        twice = jnp.where(
            left == (block % 2 == 0), here[pair : pair + 1], turned[pair : pair + 1]
        )
        usable = lax.rem(lane, capacity) < counts[block]
        high = jnp.where(usable, lax.shift_right_logical(twice, 6), 2 * LOW)
        low = jnp.where(usable, lax.bitwise_and(twice, LOW - 1), 0)
        tail = jnp.where(row == 0, high, jnp.where(row == 1, low, 0))
        tails[block] = tail.astype(jnp.float32).astype(out.dtype)
    tails_out.start()
    grads_out.wait()
    tails_out.wait()
    for copy in heads:
        copy.wait()


def packed(counts, ids, grads, weight, grad, hidden):
    blocks, width = counts.shape[0], grads.shape[1]
    capacity = grads.shape[0] // blocks
    ids = ids.reshape(-1, 128)
    return pl.pallas_call(
        pack_kernel,
        out_shape=(
            pltpu.HBM((blocks, capacity + 8, width), grads.dtype),
            pltpu.VMEM(weight.shape, weight.dtype),
            pltpu.VMEM((grad.shape[0] // 4, grad.shape[1]), grad.dtype),
            pltpu.VMEM((hidden.shape[0] // 4, hidden.shape[1]), hidden.dtype),
        ),
        in_specs=[IN_HBM] * 6,
        out_specs=(IN_HBM,) + (IN_VMEM,) * 3,
        scratch_shapes=[
            pltpu.SMEM((blocks,), jnp.int32),
            pltpu.VMEM(ids.shape, jnp.int32),
            pltpu.VMEM((blocks, capacity, width), grads.dtype),
            pltpu.VMEM((blocks, 8, width), grads.dtype),
            pltpu.SemaphoreType.DMA((8,)),
        ],
        compiler_params=pltpu.CompilerParams(vmem_limit_bytes=8 << 20),
        cost_estimate=pl.CostEstimate(flops=1000000, transcendentals=0, bytes_accessed=1 << 20),
        name="pack_rows",
    )(
        in_hbm(counts), in_hbm(ids), in_hbm(grads.reshape(blocks, capacity, width)),
        in_hbm(weight), in_hbm(grad), in_hbm(hidden),
    )


def scatter_into(core_ref, blocks, acc, out):
    rows = out.shape[0]
    wanted = core_ref[0] * rows + lax.broadcasted_iota(jnp.int32, (rows, 128), 0)
    lane = lax.broadcasted_iota(jnp.int32, (1, 128), 1)

    def ids_of(block):
        tail = blocks[block, pl.ds(64, 8), :].astype(jnp.float32)
        return (tail[0:1] * LOW + tail[1:2]).astype(jnp.int32)

    total = None if acc is None else acc[...]
    for step in range(blocks.shape[0] // 4):
        hot = []
        for block in (4 * step, 4 * step + 2):
            ids = jnp.where(lane < 64, ids_of(block), ids_of(block + 1))
            same = wanted == jnp.broadcast_to(ids, (rows, 128))
            hot.append(same.astype(jnp.float32).astype(jnp.bfloat16))
        values = blocks[pl.ds(4 * step, 4), pl.ds(0, 64), :].reshape(256, 128)
        part = jnp.dot(jnp.concatenate(hot, axis=1), values, preferred_element_type=jnp.float32)
        out[...] = part if total is None else total + part
        total = out[...]


def scatter_own_kernel(core_ref, blocks, out):
    scatter_into(core_ref, blocks, None, out)


def scatter_other_kernel(core_ref, blocks, acc, out):
    scatter_into(core_ref, blocks, acc, out)


def scattered(kernel, core, rows, blocks, *acc):
    return pl.pallas_call(
        kernel,
        out_shape=pltpu.VMEM((rows, blocks.shape[2]), jnp.float32),
        in_specs=[IN_SMEM] + [IN_VMEM] * (1 + len(acc)),
        out_specs=IN_VMEM,
        compiler_params=pltpu.CompilerParams(vmem_limit_bytes=16 << 20),
        cost_estimate=pl.CostEstimate(flops=500000000, transcendentals=0, bytes_accessed=1 << 20),
    )(core, in_vmem(blocks), *acc)


def update_kernel(core_ref, total, total_other, table, state, new_table, new_state, kept, sems):
    half = total.shape[0]
    copies = []
    for i, source in enumerate((table, state)):
        for part in range(2):
            rows = pl.ds(part * half, half)
            copies.append(
                pltpu.make_async_copy(source.at[rows, :], kept.at[i, rows, :], sems.at[i, part])
            )
    copy_all(copies)
    for copy in copies:
        copy.wait()

    def apply(place, grads):
        rows = pl.ds(pl.multiple_of(place * half, half), half)
        grad = grads[...]
        summed = kept[1, rows, :] + grad * grad
        new_state[rows, :] = summed
        new_table[rows, :] = kept[0, rows, :] - learn_rate * grad / (jnp.sqrt(summed) + epsilon)

    apply(core_ref[0], total)
    apply(1 - core_ref[0], total_other)


def updated(core, total, total_other, table, state):
    return pl.pallas_call(
        update_kernel,
        out_shape=(
            jax.ShapeDtypeStruct(table.shape, table.dtype),
            jax.ShapeDtypeStruct(state.shape, state.dtype),
        ),
        in_specs=[IN_SMEM, IN_VMEM, IN_VMEM, IN_HBM, IN_HBM],
        out_specs=(IN_VMEM, IN_VMEM),
        scratch_shapes=[
            pltpu.VMEM((2,) + table.shape, table.dtype),
            pltpu.SemaphoreType.DMA((2, 2)),
        ],
        compiler_params=pltpu.CompilerParams(vmem_limit_bytes=16 << 20),
        cost_estimate=pl.CostEstimate(flops=2000000, transcendentals=0, bytes_accessed=5 << 20),
        name="update_rows",
    )(core, total, total_other, in_hbm(table), in_hbm(state))


def copy_all(copies):
    for copy in copies:
        copy.start()


def columns_at(tile, core):
    return pl.ds(pl.multiple_of((2 * tile + core) * WIDTH, WIDTH), WIDTH)


def column_tiles(source, kept, sems, core):
    wanted = [(0, 1 - core), (1, 1 - core), (0, core), (1, core)]
    return [
        pltpu.make_async_copy(
            source.at[:, columns_at(tile, of)],
            kept.at[place // 2, :, pl.ds(place % 2 * WIDTH, WIDTH)],
            sems.at[place],
        )
        for place, (tile, of) in enumerate(wanted)
    ]


def transposed_dot(left, right):
    return lax.dot_general(left, right, ROWS_CONTRACTED, preferred_element_type=jnp.float32)


def active_of(hidden, core):
    pre = jnp.concatenate([hidden[:, columns_at(tile, core)] for tile in range(2)], axis=1)
    return jnp.maximum(pre, jnp.zeros((), pre.dtype))


def theirs_kernel(
    core_ref, grad, hidden, given, weight, grad_head, hidden_head, d_out, theirs, grad_kept,
    given_kept, hidden_kept, grad_sems, hidden_sems, given_sems,
):
    steps = grad_sems.shape[0]
    height = grad.shape[0] // steps
    core = core_ref[0]
    wide = d_out.shape[1]

    def part(source, kept, sems, i):
        rows = pl.ds(i * height, height)
        return pltpu.make_async_copy(source.at[rows, :], kept.at[rows, :], sems.at[i])

    def start_part(i):
        part(grad, grad_kept, grad_sems, i).start()
        part(hidden, hidden_kept, hidden_sems, i).start()

    def wait_part(i):
        part(grad, grad_kept, grad_sems, i).wait()
        part(hidden, hidden_kept, hidden_sems, i).wait()

    given_copies = column_tiles(given, given_kept, given_sems, core)
    start_part(1)
    start_part(2)
    for i in range(steps):
        rows = pl.ds(i * height, height)
        if i > 0:
            wait_part(i)
        if i + 3 <= steps:
            start_part((i + 3) % steps)
        given_copies[i].start()
        gradient = grad_head[...] if i == 0 else grad_kept[rows, :]
        pre = hidden_head[...] if i == 0 else hidden_kept[rows, :]
        back = lax.dot_general(
            gradient, weight[...], LANES_CONTRACTED, preferred_element_type=jnp.float32
        )
        d_out[rows, :] = jnp.where(pre > 0, back, 0.0).astype(d_out.dtype)
    wait_part(0)
    given_copies[0].wait()
    given_copies[1].wait()
    theirs[:, pl.ds(0, wide)] = transposed_dot(given_kept[0], d_out[...]).astype(theirs.dtype)
    theirs[:, pl.ds(wide, grad.shape[1])] = transposed_dot(
        active_of(hidden_kept, 1 - core), grad_kept[...]
    ).astype(theirs.dtype)
    for copy in given_copies[2:]:
        copy.wait()


def mine_kernel(core_ref, given_kept, d_hidden, hidden_kept, grad, mine):
    wide = d_hidden.shape[1]
    mine[:, pl.ds(0, wide)] = transposed_dot(given_kept[1], d_hidden[...])
    mine[:, pl.ds(wide, grad.shape[1])] = transposed_dot(
        active_of(hidden_kept, core_ref[0]), grad[...]
    )


def theirs_of(core, grad, hidden, given, weight, grad_head, hidden_head):
    tokens, steps = grad.shape[0], 4
    columns = hidden.shape[1] + grad.shape[1]
    return pl.pallas_call(
        theirs_kernel,
        out_shape=(
            pltpu.VMEM(hidden.shape, jnp.bfloat16),
            pltpu.VMEM((2 * WIDTH, columns), jnp.bfloat16),
            pltpu.VMEM(grad.shape, grad.dtype),
            pltpu.VMEM((2, tokens, 2 * WIDTH), given.dtype),
            pltpu.VMEM(hidden.shape, hidden.dtype),
        ),
        in_specs=[IN_SMEM] + [IN_HBM] * 3 + [IN_VMEM] * 3,
        out_specs=(IN_VMEM,) * 5,
        scratch_shapes=[
            pltpu.SemaphoreType.DMA((steps,)),
            pltpu.SemaphoreType.DMA((steps,)),
            pltpu.SemaphoreType.DMA((4,)),
        ],
        compiler_params=pltpu.CompilerParams(vmem_limit_bytes=24 << 20),
        cost_estimate=pl.CostEstimate(flops=5400000000, transcendentals=0, bytes_accessed=11 << 20),
        name="theirs_of",
    )(
        core, in_hbm(grad), in_hbm(hidden), in_hbm(given),
        in_vmem(weight), in_vmem(grad_head), in_vmem(hidden_head),
    )


def mine_of(core, given, d_hidden, hidden, grad):
    columns = d_hidden.shape[1] + grad.shape[1]
    return pl.pallas_call(
        mine_kernel,
        out_shape=pltpu.VMEM((2 * WIDTH, columns), jnp.float32),
        in_specs=[IN_SMEM] + [IN_VMEM] * 4,
        out_specs=IN_VMEM,
        compiler_params=pltpu.CompilerParams(vmem_limit_bytes=24 << 20),
        cost_estimate=pl.CostEstimate(flops=3200000000, transcendentals=0, bytes_accessed=2 << 20),
        name="mine_of",
    )(core, in_vmem(given), in_vmem(d_hidden), in_vmem(hidden), in_vmem(grad))


def join_kernel(mine, arrived, out, kept, sems):
    parts = sems.shape[0]
    height = mine.shape[0] // parts
    copies = []
    for part in range(parts):
        rows = pl.ds(part * height, height)
        kept[rows, :] = (mine[rows, :] + arrived[rows, :].astype(jnp.float32)).astype(kept.dtype)
        copies.append(pltpu.make_async_copy(kept.at[rows, :], out.at[rows, :], sems.at[part]))
        copies[-1].start()
    for copy in copies:
        copy.wait()


def joined(mine, arrived):
    return pl.pallas_call(
        join_kernel,
        out_shape=pltpu.HBM(mine.shape, jnp.bfloat16),
        in_specs=[IN_VMEM, IN_VMEM],
        out_specs=IN_HBM,
        scratch_shapes=[pltpu.VMEM(mine.shape, jnp.bfloat16), pltpu.SemaphoreType.DMA((8,))],
        compiler_params=pltpu.CompilerParams(vmem_limit_bytes=16 << 20),
        cost_estimate=pl.CostEstimate(flops=1000000, transcendentals=0, bytes_accessed=2 << 20),
        name="join_halves",
    )(in_vmem(mine), in_vmem(arrived))


def total_kernel(blocks, first, second):
    rows, wide = first.shape
    total = blocks[0].astype(jnp.float32)
    for pair in range(1, blocks.shape[0]):
        total += blocks[pair].astype(jnp.float32)
    total = total[:rows] + total[rows:]
    first[...] = total[:, :wide]
    second[...] = total[:, wide:]


def totals(blocks, wide):
    chips, rows, columns = blocks.shape
    return pl.pallas_call(
        total_kernel,
        out_shape=(
            jax.ShapeDtypeStruct((rows, wide), jnp.float32),
            jax.ShapeDtypeStruct((rows, columns - wide), jnp.float32),
        ),
        in_specs=[IN_VMEM],
        out_specs=(IN_VMEM, IN_VMEM),
        compiler_params=pltpu.CompilerParams(vmem_limit_bytes=16 << 20),
        cost_estimate=pl.CostEstimate(flops=1000000, transcendentals=0, bytes_accessed=2 << 20),
        name="total_blocks",
    )(in_vmem(blocks.reshape(chips // 2, 2 * rows, columns)))


def to_owners(share):
    chips = lax.axis_size(CHIPS)
    blocks = share.reshape(chips, share.shape[0] // chips, share.shape[1])
    return lax.all_to_all(blocks, CHIPS, 0, 0, tiled=True)


def on_device(
    layer_input,
    hidden_pre,
    out_grad,
    second_weight,
    row_grads,
    row_ids,
    block_counts,
    emb_table,
    adagrad_state,
):
    at_core = lax.axis_index("c").astype(jnp.int32).reshape(1)
    message, *heads = packed(block_counts, row_ids, row_grads, second_weight, out_grad, hidden_pre)
    own = lax.all_to_all(message, DEV, 0, 0, tiled=True)

    d_hidden, theirs, grad_kept, given_kept, hidden_kept = theirs_of(
        at_core, out_grad, hidden_pre, layer_input, *heads
    )
    arrived = lax.ppermute(theirs, "c", SWAP)
    mine = mine_of(at_core, given_kept, d_hidden, hidden_kept, grad_kept)
    share = joined(mine, arrived)
    blocks = to_owners(share)
    grad_first, grad_second = totals(blocks, hidden_pre.shape[1])

    other = lax.ppermute(own, "c", SWAP)
    half = emb_table.shape[0] // 2
    near = scattered(scatter_own_kernel, at_core, half, own)
    near = scattered(scatter_other_kernel, at_core, half, other, near)
    near = lax.optimization_barrier(near.astype(jnp.float16))
    far = lax.ppermute(near, "zh", SWAP)
    total = near.astype(jnp.float32) + far.astype(jnp.float32)
    total_other = lax.ppermute(total, "c", SWAP)
    new_table, new_state = updated(at_core, total, total_other, emb_table, adagrad_state)
    return (grad_first, grad_second, new_table, new_state)


def solution(mesh):
    names = ("zh", "c", "y", "x", "zl")
    split = Mesh(mesh.devices.reshape(2, 2, 4, 4, 2), names)
    every = P(names, None)
    in_specs = (
        every,
        every,
        every,
        P(),
        every,
        P(names),
        P(names),
        P(DEV, None),
        P(DEV, None),
    )
    out_specs = (every, every, P(DEV, None), P(DEV, None))
    return jax.shard_map(
        on_device, mesh=split, in_specs=in_specs, out_specs=out_specs, check_vma=False
    )
```
